512 devices in a mesh: mic: 128 (over z_hi, x, y, core), tile: 4 (over z_lo).
Axes of the slice: x: 4, y: 8, z: 8 (z_hi: 2, z_lo: 4; z = z_hi * 4 + z_lo), core: 2. Of those that a mesh axis runs over, the one named last changes fastest.
Arguments:
- micrograph: bfloat16 [128, 447, 1536], P('mic', None, 'tile'), may hold values from -6 to 6
- templates: bfloat16 [128, 384, 384], P('mic'), may hold values from -6 to 6
- orient_ids: int32 [128], P('mic'), may hold values from 0 to 359
- defocus_bins: int32 [128], P('mic'), may hold values from 0 to 15
Outputs:
- peak_value: float32 [128, 64, 1536], P('mic', None, 'tile')
- corr_sum: float32 [128, 64, 1536], P('mic', None, 'tile')
- corr_sumsq: float32 [128, 64, 1536], P('mic', None, 'tile')
- orient_cos: float32 [128, 64, 1536], P('mic', None, 'tile')
- orient_sin: float32 [128, 64, 1536], P('mic', None, 'tile')
The draws below stay inside these ranges and needn't reach their ends.
All inputs are finite; a program needn't handle non-finite values.
Results may differ from the reference program's by a relative error of at most 0.013.
Values may be sent and summed in bfloat16 or wider, within the bound.
A program may use at most 64 MiB of HBM per device.

```python
import math
import jax
import jax.numpy as jnp
from jax import lax

TS = 384
TC = 384
MH = 64
STEPS = 4
NANG = 360
NBINS = 16
MICS = 128
NCOL = 1536
MR = 447
MC = 767
LR = 448
LC = 768
HALF = 384
N_TILE = 4


def place_ends(result, key, low, high):
    longest = result.shape.index(max(result.shape))
    spots = []
    for shift in (0, 1):
        where = [jax.random.randint(jax.random.fold_in(key, axis), (), 0, length) for axis, length in enumerate(result.shape)]
        where[longest] = (where[longest] + shift) % result.shape[longest]
        spots.append(tuple(where))
    return result.at[spots[0]].set(low).at[spots[1]].set(high)


def block_levels(stream_key, shape, cuts, least, high):
    level = 1.0
    for dim, blocks in cuts:
        heights = jax.random.uniform(jax.random.fold_in(jax.random.fold_in(stream_key, 6), dim), (blocks,), jnp.float32, least / len(cuts), high / len(cuts))
        level = level * jnp.repeat(jnp.exp(heights), shape[dim] // blocks).reshape((-1,) + (1,) * (len(shape) - 1 - dim))
    return level


def noise(own_key, dims, scale, reach, cuts=(), kind=jnp.bfloat16):
    entries = jax.random.normal(own_key, dims, jnp.float32) * scale
    if len(cuts) > 0:
        entries = block_levels(own_key, dims, cuts, -0.22, 0.18) * entries
    return jnp.clip(entries, min=-reach, max=reach).astype(kind)


def setup_inputs(seed: int = 0) -> dict:
    splits = jax.random.split(jax.random.key(seed), 5)
    return {
        "micrograph": noise(splits[0], (MICS, MR, NCOL), 1.0, 6.0, ((0, 128), (2, 4))),
        "templates": noise(splits[1], (MICS, TS, TS), 1.0, 6.0, ((0, 128),)),
        "orient_ids": place_ends(jax.random.randint(splits[2], (MICS,), 0, NANG), jax.random.fold_in(splits[2], 1), 0, NANG - 1).astype(jnp.int32),
        "defocus_bins": place_ends(jax.random.randint(splits[3], (MICS,), 0, NBINS), jax.random.fold_in(splits[3], 1), 0, NBINS - 1).astype(jnp.int32),
    }


AMPLITUDE = 0.07
WAVELENGTH = 0.0197
BASE_DEFOCUS = 8000.0
DEFOCUS_STEP = 1000.0

def counting(length):
    return jnp.arange(length, dtype=jnp.int32)

def trig_pair(left_ids, right_ids, length):
    product_ids = left_ids[:, None] * right_ids[None, :] % length
    angles = product_ids.astype(jnp.float32) * (2.0 * math.pi / length)
    return (jnp.cos(angles).astype(jnp.bfloat16), jnp.sin(angles).astype(jnp.bfloat16))

def forward_columns(height, breadth, length):
    cosine, sine_part = trig_pair(counting(height), counting(breadth), length)
    return jnp.concatenate([cosine, -sine_part], axis=1)

def inverse_columns(breadth, height, length):
    cosine, sine_part = trig_pair(counting(breadth), counting(height), length)
    weights = jnp.where(counting(breadth) == 0, 1.0, 2.0).astype(jnp.bfloat16)[:, None]
    return jnp.concatenate([cosine * weights, -sine_part * weights], axis=0)

def stacked_rows(left_ids, right_ids, length):
    cosine, sine_part = trig_pair(left_ids, right_ids, length)
    return jnp.concatenate([cosine, sine_part], axis=0)

def complex_left(stacked, values, direction):
    product = jnp.dot(stacked, values, preferred_element_type=jnp.float32)
    height = stacked.shape[0] // 2
    breadth = values.shape[1] // 2
    upper_part = product[:height]
    lower_part = product[height:]
    real_part = upper_part[:, :breadth] - direction * lower_part[:, breadth:]
    imag_part = upper_part[:, breadth:] + direction * lower_part[:, :breadth]
    return jnp.concatenate([real_part, imag_part], axis=1)

def transfer_function(bin_value, rows_length, breadth, cols_length):
    row_ids = counting(rows_length)
    folded = (row_ids + rows_length // 2) % rows_length - rows_length // 2
    freq_rows = folded.astype(jnp.float32) / rows_length
    freq_cols = counting(breadth).astype(jnp.float32) / cols_length
    radius = freq_rows[:, None] * freq_rows[:, None] + freq_cols[None, :] * freq_cols[None, :]
    defocus = BASE_DEFOCUS + DEFOCUS_STEP * bin_value.astype(jnp.float32)
    phases = math.pi * WAVELENGTH * defocus * radius
    return -(math.sqrt(1.0 - AMPLITUDE * AMPLITUDE) * jnp.sin(phases) + AMPLITUDE * jnp.cos(phases))

def angle_pairs(orient_ids):
    angles = orient_ids.astype(jnp.float32) * (2.0 * math.pi / NANG)
    return jnp.stack([jnp.cos(angles), jnp.sin(angles)], axis=-1).astype(jnp.bfloat16)

def micro_spectrum(micro_strip, col_forward, row_forward, ctf_values):
    spectrum_cols = jnp.dot(micro_strip, col_forward, preferred_element_type=jnp.float32).astype(jnp.bfloat16)
    spectrum = complex_left(row_forward, spectrum_cols, -1.0)
    return (spectrum * jnp.concatenate([ctf_values, ctf_values], axis=1)).astype(jnp.bfloat16)

def template_spectrum(template, col_forward, row_forward):
    template_cols = jnp.dot(template, col_forward[:template.shape[1]], preferred_element_type=jnp.float32).astype(jnp.bfloat16)
    return complex_left(row_forward, template_cols, -1.0).astype(jnp.bfloat16)

def spectral_product(micro_rows, template_rows):
    breadth = micro_rows.shape[1] // 2
    micro_real = micro_rows[:, :breadth].astype(jnp.float32)
    micro_imag = micro_rows[:, breadth:].astype(jnp.float32)
    tmpl_real = template_rows[:, :breadth].astype(jnp.float32)
    tmpl_imag = template_rows[:, breadth:].astype(jnp.float32)
    real_part = micro_real * tmpl_real + micro_imag * tmpl_imag
    imag_part = micro_imag * tmpl_real - micro_real * tmpl_imag
    return jnp.concatenate([real_part, imag_part], axis=1).astype(jnp.bfloat16)

def accumulate(statistics, correlation, angle_pair):
    weight = jax.nn.softplus(2.0 * correlation)
    cos_value = angle_pair[0].astype(jnp.float32)
    sin_value = angle_pair[1].astype(jnp.float32)
    fresh = (correlation, correlation, correlation * correlation, weight, weight * cos_value, weight * sin_value)
    if statistics is None:
        return fresh
    return (jnp.maximum(statistics[0], fresh[0]), statistics[1] + fresh[1], statistics[2] + fresh[2], statistics[3] + fresh[3], statistics[4] + fresh[4], statistics[5] + fresh[5])

def finish(statistics):
    return (statistics[0], statistics[1], statistics[2], statistics[4] / statistics[3], statistics[5] / statistics[3])

def reference(micrograph, templates, orient_ids, defocus_bins):
    col_forward = forward_columns(MC, HALF, LC)
    row_forward = stacked_rows(counting(LR), counting(MR), LR)
    row_template = stacked_rows(counting(LR), counting(TS), LR)
    row_inverse = stacked_rows(counting(MH), counting(LR), LR)
    col_inverse = inverse_columns(HALF, TC, LC)
    norm_scale = 1.0 / (TS * LR * LC)

    def one_template(template):
        return template_spectrum(template, col_forward, row_template)
    spectra = lax.map(one_template, templates)
    angles_all = angle_pairs(orient_ids)
    padded = jnp.pad(micrograph, ((0, 0), (0, 0), (0, TS - 1)))

    def one_micrograph(micro_index):
        ctf_values = transfer_function(defocus_bins[micro_index], LR, HALF, LC)
        rows_all = lax.dynamic_index_in_dim(padded, micro_index, 0, keepdims=False)
        pieces = []
        for tile_index in range(N_TILE):
            micro_strip = rows_all[:, tile_index * TC:tile_index * TC + MC]
            micro_spec = micro_spectrum(micro_strip, col_forward, row_forward, ctf_values)
            statistics = None
            for step_index in range(STEPS):
                target = (micro_index + step_index) % MICS
                template_spec = lax.dynamic_index_in_dim(spectra, target, 0, keepdims=False)
                angle_pair = lax.dynamic_index_in_dim(angles_all, target, 0, keepdims=False)
                product = spectral_product(micro_spec, template_spec)
                inverse_rows = complex_left(row_inverse, product, 1.0).astype(jnp.bfloat16)
                correlation = jnp.dot(inverse_rows, col_inverse, preferred_element_type=jnp.float32) * norm_scale
                statistics = accumulate(statistics, correlation, angle_pair)
            pieces.append(finish(statistics))
        return tuple((jnp.concatenate([tile_stats[position] for tile_stats in pieces], axis=1) for position in range(5)))
    outputs = lax.map(one_micrograph, counting(MICS))
    return (outputs[0], outputs[1], outputs[2], outputs[3], outputs[4])
```

```python
import functools
import math

import jax
import jax.numpy as jnp
import ml_dtypes
import numpy as np
from jax import lax
from jax.experimental import pallas as pl
from jax.experimental.pallas import tpu as pltpu
from jax.sharding import PartitionSpec as P

TS = 384
TC = 384
MH = 64
STEPS = 4
NANG = 360
NBINS = 16
MR = 447
MC = 767
LR = 448
LC = 768
HALF = 384
FOLD = 225
FR = 240
NB = 3
LB = 128
SLOT = 400
CHUNKS = ((0, 128), (128, 128), (256, 144))
NCH = len(CHUNKS)

AMPLITUDE = 0.07
WAVELENGTH = 0.0197
BASE_DEFOCUS = 8000.0
DEFOCUS_STEP = 1000.0
MESH = pl.DeviceIdType.MESH
BF16 = jnp.bfloat16
F32 = jnp.float32


def trig(left, right, length):
    ids = (np.arange(left)[:, None] * np.arange(right)[None, :]) % length
    angles = ids.astype(np.float32) * np.float32(2.0 * math.pi / length)
    return np.cos(angles), np.sin(angles)


def tables():
    bf16 = ml_dtypes.bfloat16
    c, s = trig(LC, HALF, LC)
    c[MC:], s[MC:] = 0.0, 0.0
    colf = np.stack([np.concatenate([c[:, j * LB:(j + 1) * LB], -s[:, j * LB:(j + 1) * LB]], 1) for j in range(NB)])
    c, s = trig(FOLD, LR, LR)
    rowf = np.zeros((2 * FR, LR), np.float32)
    rowf[:FOLD, :MR] = c[:, :MR]
    rowf[FR:FR + FOLD, :MR] = s[:, :MR]
    c, s = trig(MH, FOLD, LR)
    rowi = np.zeros((2 * MH, 2 * FR), np.float32)
    rowi[:MH, :FOLD] = c
    rowi[MH:, :FOLD] = s
    rowi[:MH, FR + 1:FR + FOLD - 1] = c[:, 1:FOLD - 1]
    rowi[MH:, FR + 1:FR + FOLD - 1] = -s[:, 1:FOLD - 1]
    c, s = trig(HALF, TC, LC)
    w = np.where(np.arange(HALF) == 0, 1.0, 2.0).astype(np.float32)[:, None]
    c, s = c * w, s * w
    coli = np.stack([np.concatenate([c[j * LB:(j + 1) * LB], -s[j * LB:(j + 1) * LB]], 0) for j in range(NB)])
    scale = math.pi * WAVELENGTH * (BASE_DEFOCUS + DEFOCUS_STEP * np.arange(NBINS))
    phi = math.atan2(AMPLITUDE, math.sqrt(1.0 - AMPLITUDE * AMPLITUDE))
    rows = scale[None, :] * (np.arange(FOLD)[:, None] / LR) ** 2 + phi
    rtab = np.zeros((FR, 128), np.float32)
    rtab[:FOLD, :NBINS] = -np.sin(rows)
    rtab[:FOLD, NBINS:2 * NBINS] = -np.cos(rows)
    cols = scale[:, None] * (np.arange(HALF)[None, :] / LC) ** 2
    ctab = np.concatenate([np.cos(cols), np.sin(cols)], 0).astype(np.float32)
    return (colf.astype(bf16), rowf.astype(bf16), rowi.astype(bf16), coli.astype(bf16), rtab, ctab)


def kernel(mics, tiles, mic_ref, tmpl_ref, orient_ref, bins_ref, colf_h, rowf_h, rowi_h, coli_h, rtab_h, ctab_h,
           out_ref, colf, rowf, rowi, coli, rtab, ctab, own, halo, slots, xown, xs, mspec, tbuf, tcs, prod,
           lsem, hsend, hrecv, ssem, rsem):
    m = lax.axis_index("mic")
    p = lax.axis_index("tile")
    group = mics // 2
    mg = lax.rem(m, group)
    odd = lax.rem(m, 2)
    even = 1 - odd
    sib = m + 1 - 2 * odd
    down1 = lax.rem(m + mics - 1, mics)
    down2 = lax.rem(m + mics - 2, mics)
    up1 = lax.rem(m + 1, mics)
    up2 = lax.rem(m + 2, mics)
    last = tiles - 1
    edge_tile = jnp.logical_or(p == 0, p == last)
    low2 = mg < 2
    low1 = mg == 0
    high2 = mg >= group - 2
    high1 = mg == group - 1
    inner = jnp.logical_and(p > 0, p < last)
    chain_p = p < last - 1

    own_go = jnp.logical_or(jnp.logical_not(low2), edge_tile)
    own_to = (down2, jnp.where(low2, last - p, p))
    fwd_go = jnp.logical_and(even == 1, jnp.logical_or(jnp.logical_not(low1), edge_tile))
    fwd_to = (down1, jnp.where(low1, last - p, p))
    chain2 = jnp.logical_and(high2, chain_p)
    chain3 = jnp.logical_and(high1, chain_p)
    halo_go = p > 0
    halo_come = p < last
    next_tile = jnp.minimum(p + 1, last)
    prev_tile = jnp.maximum(p - 1, 0)

    loads = [
        pltpu.make_async_copy(tmpl_ref.at[0], slots.at[0, pl.ds(0, TS)], lsem.at[0]),
        pltpu.make_async_copy(mic_ref.at[0], own, lsem.at[1]),
        pltpu.make_async_copy(colf_h, colf, lsem.at[2]),
        pltpu.make_async_copy(rowf_h, rowf, lsem.at[3]),
        pltpu.make_async_copy(rtab_h, rtab, lsem.at[4]),
        pltpu.make_async_copy(ctab_h, ctab, lsem.at[5]),
        pltpu.make_async_copy(rowi_h, rowi, lsem.at[6]),
        pltpu.make_async_copy(coli_h, coli, lsem.at[7]),
    ]
    for load in loads:
        load.start()

    barrier = pltpu.get_barrier_semaphore()

    def greet(to):
        pl.semaphore_signal(barrier, inc=1, device_id=to, device_id_type=MESH)

    greet((sib, p))
    inner_high2 = jnp.logical_and(high2, inner)
    inner_high1 = jnp.logical_and(high1, inner)

    @pl.when(inner_high2)
    def _():
        greet((m, prev_tile))

    @pl.when(jnp.logical_not(inner_high2))
    def _():
        greet((up2, jnp.where(high2, last - p, p)))

    @pl.when(inner_high1)
    def _():
        greet((m, prev_tile))

    @pl.when(jnp.logical_and(odd == 1, jnp.logical_not(inner_high1)))
    def _():
        greet((up1, jnp.where(high1, last - p, p)))

    @pl.when(halo_come)
    def _():
        greet((m, next_tile))

    @pl.when(jnp.logical_not(halo_come))
    def _():
        halo[...] = jnp.zeros_like(halo)

    angle = jnp.full((16, TS), orient_ref[0], jnp.int32).astype(F32) * (2.0 * math.pi / NANG)
    upper = lax.broadcasted_iota(jnp.int32, (16, TS), 0) < 8
    slots[0, TS:, :] = jnp.where(upper, jnp.cos(angle), jnp.sin(angle)).astype(BF16)

    i32 = lambda b: b.astype(jnp.int32)
    pl.semaphore_wait(barrier, 1 + i32(own_go) + i32(fwd_go) + i32(halo_go) + i32(chain2) + i32(chain3))

    def halo_copy():
        return pltpu.make_async_remote_copy(
            src_ref=mic_ref.at[0], dst_ref=halo, send_sem=hsend, recv_sem=hrecv,
            device_id=(m, prev_tile), device_id_type=MESH)

    def piece(src, dst, sem, chunk, to):
        start, rows = CHUNKS[chunk]
        return pltpu.make_async_remote_copy(
            src_ref=slots.at[src, pl.ds(start, rows)], dst_ref=slots.at[dst, pl.ds(start, rows)],
            send_sem=ssem.at[sem, chunk], recv_sem=rsem.at[dst - 1, chunk],
            device_id=to, device_id_type=MESH)

    def arrived(slot, chunk):
        piece(slot, slot, 0, chunk, (sib, p)).wait_recv()

    @pl.when(halo_go)
    def _():
        halo_copy().start()

    loads[0].wait()

    @pl.when(own_go)
    def _():
        for c in range(NCH):
            piece(0, 2, 0, c, own_to).start()

    @pl.when(odd == 1)
    def _():
        for c in range(NCH):
            piece(0, 1, 1, c, (sib, p)).start()

    def forward2(c):
        arrived(2, c)

        @pl.when(fwd_go)
        def _():
            piece(2, 3, 3, c, fwd_to).start()

        @pl.when(odd == 1)
        def _():
            piece(2, 3, 2, c, (sib, p)).start()

        @pl.when(even == 1)
        def _():
            piece(2, 1, 2, c, (sib, p)).start()

        @pl.when(chain2)
        def _():
            piece(2, 2, 4, c, (m, next_tile)).start()

    def forward3(c):
        arrived(3, c)

        @pl.when(chain3)
        def _():
            piece(3, 3, 5, c, (m, next_tile)).start()

    def spectrum(values, block, table_rows):
        both = jnp.dot(table_rows, values, preferred_element_type=F32)
        cr, ci = both[:FR, :LB], both[:FR, LB:]
        sr, si = both[FR:, :LB], both[FR:, LB:]
        return cr + si, ci - sr, cr - si, ci + sr

    def tspec(s):
        for j in range(NB):
            tcs[j] = jnp.dot(slots[s, :TS, :], colf[j, :TS, :], preferred_element_type=F32).astype(BF16)
            ar, ai, br, bi = spectrum(tcs[j], j, rowf[:, :TS])
            tbuf[s, j, :FR, :LB] = ar
            tbuf[s, j, :FR, LB:] = ai
            tbuf[s, j, FR:, :LB] = br
            tbuf[s, j, FR:, LB:] = bi

    def match(s, first):
        corr = None
        for j in range(NB):
            mr, mi = mspec[j, :, :LB], mspec[j, :, LB:]
            tr, ti = tbuf[s, j, :, :LB], tbuf[s, j, :, LB:]
            prod[j, :, :LB] = (mr * tr + mi * ti).astype(BF16)
            prod[j, :, LB:] = (mi * tr - mr * ti).astype(BF16)
            both = jnp.dot(rowi[...], prod[j], preferred_element_type=F32)
            real = both[:MH, :LB] - both[MH:, LB:]
            imag = both[:MH, LB:] + both[MH:, :LB]
            back = jnp.concatenate([real, imag], axis=1).astype(BF16)
            part = jnp.dot(back, coli[j], preferred_element_type=F32)
            corr = part if corr is None else corr + part
        corr = corr * (1.0 / (TS * LR * LC))
        x = 2.0 * corr
        weight = jnp.maximum(x, 0.0) + jnp.log1p(jnp.exp(-jnp.abs(x)))
        pair = slots[s, TS:, :].astype(F32)
        wc, ws = weight * pair[0:1], weight * pair[8:9]
        if first:
            fresh = (corr, corr, corr * corr, weight, wc, ws)
        else:
            fresh = (jnp.maximum(out_ref[0], corr), out_ref[1] + corr, out_ref[2] + corr * corr,
                     out_ref[3] + weight, out_ref[4] + wc, out_ref[5] + ws)
        for n, value in enumerate(fresh):
            out_ref[n] = value

    for load in loads[1:]:
        load.wait()
    for j in range(NB):
        xown[j, LR - 8:, :] = jnp.zeros((8, 2 * LB), F32)
        xown[j, :MR, :] = jnp.dot(own[...], colf[j, :TS, :], preferred_element_type=F32)
    tspec(0)
    forward2(0)

    @pl.when(even == 1)
    def _():
        for c in range(NCH):
            arrived(1, c)
        tspec(1)

    for c in range(1, NCH):
        forward2(c)
    tspec(2)

    @pl.when(halo_come)
    def _():
        halo_copy().wait_recv()
    bin_id = bins_ref[0]
    lane = lax.broadcasted_iota(jnp.int32, (FR, 128), 1)
    rs = jnp.sum(jnp.where(lane == bin_id, rtab[...], 0.0), axis=1, keepdims=True)
    rc = jnp.sum(jnp.where(lane == bin_id + NBINS, rtab[...], 0.0), axis=1, keepdims=True)
    which = lax.broadcasted_iota(jnp.int32, (2 * NBINS, HALF), 0)
    cc = jnp.sum(jnp.where(which == bin_id, ctab[...], 0.0), axis=0, keepdims=True)
    cs = jnp.sum(jnp.where(which == bin_id + NBINS, ctab[...], 0.0), axis=0, keepdims=True)
    for j in range(NB):
        xown[j, :MR, :] = xown[j, :MR, :] + jnp.dot(halo[...], colf[j, TS:, :], preferred_element_type=F32)
        xs[j] = xown[j].astype(BF16)
        ctf = rs * cc[:, j * LB:(j + 1) * LB] + rc * cs[:, j * LB:(j + 1) * LB]
        ar, ai, br, bi = spectrum(xs[j], j, rowf[...])
        mspec[j, :FR, :LB] = ar * ctf
        mspec[j, :FR, LB:] = ai * ctf
        mspec[j, FR:, :LB] = br * ctf
        mspec[j, FR:, LB:] = bi * ctf

    forward3(0)
    match(0, True)
    match(2, False)

    @pl.when(odd == 1)
    def _():
        for c in range(NCH):
            arrived(1, c)
        tspec(1)

    match(1, False)
    for c in range(1, NCH):
        forward3(c)
    tspec(3)
    match(3, False)

    @pl.when(halo_go)
    def _():
        halo_copy().wait_send()

    for go, src, dst, sem, to in (
        (own_go, 0, 2, 0, own_to), (odd == 1, 0, 1, 1, (sib, p)), (fwd_go, 2, 3, 3, fwd_to),
        (odd == 1, 2, 3, 2, (sib, p)), (even == 1, 2, 1, 2, (sib, p)),
        (chain2, 2, 2, 4, (m, next_tile)), (chain3, 3, 3, 5, (m, next_tile)),
    ):
        @pl.when(go)
        def _(src=src, dst=dst, sem=sem, to=to):
            for c in range(NCH):
                piece(src, dst, sem, c, to).wait_send()


def body(mics, tiles, consts, micrograph, templates, orient_ids, defocus_bins):
    hbm = pl.BlockSpec(memory_space=pl.ANY)
    smem = pl.BlockSpec(memory_space=pltpu.SMEM)
    stats = pl.pallas_call(
        functools.partial(kernel, mics, tiles),
        out_shape=jax.ShapeDtypeStruct((6, MH, TC), F32),
        in_specs=[hbm, hbm, smem, smem] + [hbm] * 6,
        out_specs=pl.BlockSpec(memory_space=pltpu.VMEM),
        scratch_shapes=[
            pltpu.VMEM((NB, LC, 2 * LB), BF16),
            pltpu.VMEM((2 * FR, LR), BF16),
            pltpu.VMEM((2 * MH, 2 * FR), BF16),
            pltpu.VMEM((NB, 2 * LB, TC), BF16),
            pltpu.VMEM((FR, 128), F32),
            pltpu.VMEM((2 * NBINS, HALF), F32),
            pltpu.VMEM((MR, TC), BF16),
            pltpu.VMEM((MR, TC), BF16),
            pltpu.VMEM((STEPS, SLOT, TS), BF16),
            pltpu.VMEM((NB, LR, 2 * LB), F32),
            pltpu.VMEM((NB, LR, 2 * LB), BF16),
            pltpu.VMEM((NB, 2 * FR, 2 * LB), F32),
            pltpu.VMEM((STEPS, NB, 2 * FR, 2 * LB), F32),
            pltpu.VMEM((NB, TS, 2 * LB), BF16),
            pltpu.VMEM((NB, 2 * FR, 2 * LB), BF16),
            pltpu.SemaphoreType.DMA((8,)),
            pltpu.SemaphoreType.DMA,
            pltpu.SemaphoreType.DMA,
            pltpu.SemaphoreType.DMA((6, NCH)),
            pltpu.SemaphoreType.DMA((3, NCH)),
        ],
        compiler_params=pltpu.CompilerParams(
            collective_id=0, has_side_effects=True, vmem_limit_bytes=48 * 1024 * 1024),
    )(micrograph, templates, orient_ids, defocus_bins, *consts)
    results = (stats[0], stats[1], stats[2], stats[4] / stats[3], stats[5] / stats[3])
    return tuple(value[None] for value in results)


def solution(mesh):
    placed = (P("mic", None, "tile"), P("mic", None, None), P("mic"), P("mic"))
    consts = tuple(jnp.asarray(table) for table in tables())
    return jax.shard_map(
        functools.partial(body, mesh.shape["mic"], mesh.shape["tile"], consts),
        mesh=mesh,
        in_specs=placed,
        out_specs=(P("mic", None, "tile"),) * 5,
        check_vma=False,
    )
```

```python
import functools
import math

import jax
import jax.numpy as jnp
import ml_dtypes
import numpy as np
from jax import lax
from jax.experimental import pallas as pl
from jax.experimental.pallas import tpu as pltpu
from jax.sharding import PartitionSpec as P

TS = 384
TC = 384
MH = 64
STEPS = 4
NANG = 360
NBINS = 16
MR = 447
MC = 767
LR = 448
LC = 768
HALF = 384
FOLD = 225
FR = 240
NB = 3
LB = 128
SLOT = 400
CHUNKS = ((0, 64), (64, 64), (128, 64), (192, 64), (256, 64), (320, 80))
NCH = len(CHUNKS)

AMPLITUDE = 0.07
WAVELENGTH = 0.0197
BASE_DEFOCUS = 8000.0
DEFOCUS_STEP = 1000.0
MESH = pl.DeviceIdType.MESH
BF16 = jnp.bfloat16
F32 = jnp.float32


def trig(left, right, length):
    ids = (np.arange(left)[:, None] * np.arange(right)[None, :]) % length
    angles = ids.astype(np.float32) * np.float32(2.0 * math.pi / length)
    return np.cos(angles), np.sin(angles)


def tables():
    bf16 = ml_dtypes.bfloat16
    c, s = trig(LC, HALF, LC)
    c[MC:], s[MC:] = 0.0, 0.0
    colf = np.stack([np.concatenate([c[:, j * LB:(j + 1) * LB], -s[:, j * LB:(j + 1) * LB]], 1) for j in range(NB)])
    c, s = trig(FOLD, LR, LR)
    rowf = np.zeros((2 * FR, LR), np.float32)
    rowf[:FOLD, :MR] = c[:, :MR]
    rowf[FR:FR + FOLD, :MR] = s[:, :MR]
    c, s = trig(MH, FOLD, LR)
    rowi = np.zeros((2 * MH, 2 * FR), np.float32)
    rowi[:MH, :FOLD] = c
    rowi[MH:, :FOLD] = s
    rowi[:MH, FR + 1:FR + FOLD - 1] = c[:, 1:FOLD - 1]
    rowi[MH:, FR + 1:FR + FOLD - 1] = -s[:, 1:FOLD - 1]
    c, s = trig(HALF, TC, LC)
    w = np.where(np.arange(HALF) == 0, 1.0, 2.0).astype(np.float32)[:, None]
    c, s = c * w, s * w
    coli = np.stack([np.concatenate([c[j * LB:(j + 1) * LB], -s[j * LB:(j + 1) * LB]], 0) for j in range(NB)])
    scale = math.pi * WAVELENGTH * (BASE_DEFOCUS + DEFOCUS_STEP * np.arange(NBINS))
    phi = math.atan2(AMPLITUDE, math.sqrt(1.0 - AMPLITUDE * AMPLITUDE))
    rows = scale[None, :] * (np.arange(FOLD)[:, None] / LR) ** 2 + phi
    rtab = np.zeros((FR, 128), np.float32)
    rtab[:FOLD, :NBINS] = -np.sin(rows)
    rtab[:FOLD, NBINS:2 * NBINS] = -np.cos(rows)
    cols = scale[:, None] * (np.arange(HALF)[None, :] / LC) ** 2
    ctab = np.concatenate([np.cos(cols), np.sin(cols)], 0).astype(np.float32)
    return (colf.astype(bf16), rowf.astype(bf16), rowi.astype(bf16), coli.astype(bf16), rtab, ctab)


def kernel(mics, tiles, mic_ref, tmpl_ref, orient_ref, bins_ref, colf_h, rowf_h, rowi_h, coli_h, rtab_h, ctab_h,
           out_ref, colf, rowf, rowi, coli, rtab, ctab, own, halo, slots, urow, trow, mspec, tbuf, prod,
           lsem, hsend, hrecv, ssem, rsem):
    m = lax.axis_index("mic")
    p = lax.axis_index("tile")
    group = mics // 2
    mg = lax.rem(m, group)
    odd = lax.rem(m, 2)
    even = 1 - odd
    sib = m + 1 - 2 * odd
    down1 = lax.rem(m + mics - 1, mics)
    down2 = lax.rem(m + mics - 2, mics)
    up1 = lax.rem(m + 1, mics)
    up2 = lax.rem(m + 2, mics)
    last = tiles - 1
    upper_half = m >= group
    low2 = mg < 2
    low1 = mg == 0
    high2 = mg >= group - 2
    high1 = mg == group - 1

    edge_tile = jnp.logical_or(p == 0, p == last)
    exit_tile = edge_tile
    entry_tile = edge_tile
    chain_next = jnp.where(p == 0, 1, last - 1)
    chain_prev = jnp.where(p == 1, 0, last)
    chain_p = edge_tile
    own_go = jnp.logical_or(jnp.logical_not(low2), exit_tile)
    own_to = (down2, jnp.where(low2, last - p, p))
    fwd_go = jnp.logical_and(even == 1, jnp.logical_or(jnp.logical_not(low1), exit_tile))
    fwd_to = (down1, jnp.where(low1, last - p, p))
    chain2 = jnp.logical_and(high2, chain_p)
    chain3 = jnp.logical_and(high1, chain_p)
    halo_go = p > 0
    halo_come = p < last
    next_tile = jnp.minimum(p + 1, last)
    prev_tile = jnp.maximum(p - 1, 0)

    loads = [
        pltpu.make_async_copy(tmpl_ref.at[0], slots.at[0, pl.ds(0, TS)], lsem.at[0]),
        pltpu.make_async_copy(mic_ref.at[0], own, lsem.at[1]),
        pltpu.make_async_copy(colf_h, colf, lsem.at[2]),
        pltpu.make_async_copy(rowf_h, rowf, lsem.at[3]),
        pltpu.make_async_copy(rtab_h, rtab, lsem.at[4]),
        pltpu.make_async_copy(ctab_h, ctab, lsem.at[5]),
        pltpu.make_async_copy(rowi_h, rowi, lsem.at[6]),
        pltpu.make_async_copy(coli_h, coli, lsem.at[7]),
    ]
    for load in loads:
        load.start()

    barrier = pltpu.get_barrier_semaphore()

    def greet(to):
        pl.semaphore_signal(barrier, inc=1, device_id=to, device_id_type=MESH)

    greet((sib, p))
    inner_high2 = jnp.logical_and(high2, jnp.logical_not(entry_tile))
    inner_high1 = jnp.logical_and(high1, jnp.logical_not(entry_tile))

    @pl.when(inner_high2)
    def _():
        greet((m, chain_prev))

    @pl.when(jnp.logical_not(inner_high2))
    def _():
        greet((up2, jnp.where(high2, last - p, p)))

    @pl.when(inner_high1)
    def _():
        greet((m, chain_prev))

    @pl.when(jnp.logical_and(odd == 1, jnp.logical_not(inner_high1)))
    def _():
        greet((up1, jnp.where(high1, last - p, p)))

    @pl.when(halo_come)
    def _():
        greet((m, next_tile))

    @pl.when(jnp.logical_not(halo_come))
    def _():
        halo[...] = jnp.zeros_like(halo)

    angle = jnp.full((16, TS), orient_ref[0], jnp.int32).astype(F32) * (2.0 * math.pi / NANG)
    upper = lax.broadcasted_iota(jnp.int32, (16, TS), 0) < 8
    slots[0, TS:, :] = jnp.where(upper, jnp.cos(angle), jnp.sin(angle)).astype(BF16)

    i32 = lambda b: b.astype(jnp.int32)
    pl.semaphore_wait(barrier, 1 + i32(own_go) + i32(fwd_go) + i32(halo_go) + i32(chain2) + i32(chain3))

    def halo_copy():
        return pltpu.make_async_remote_copy(
            src_ref=mic_ref.at[0], dst_ref=halo, send_sem=hsend, recv_sem=hrecv,
            device_id=(m, prev_tile), device_id_type=MESH)

    def piece(src, dst, sem, chunk, to):
        start, rows = CHUNKS[chunk]
        return pltpu.make_async_remote_copy(
            src_ref=slots.at[src, pl.ds(start, rows)], dst_ref=slots.at[dst, pl.ds(start, rows)],
            send_sem=ssem.at[sem, chunk], recv_sem=rsem.at[dst - 1, chunk],
            device_id=to, device_id_type=MESH)

    def arrived(slot, chunk):
        piece(slot, slot, 0, chunk, (sib, p)).wait_recv()

    @pl.when(halo_go)
    def _():
        halo_copy().start()

    loads[0].wait()

    @pl.when(own_go)
    def _():
        for c in range(NCH):
            piece(0, 2, 0, c, own_to).start()

    @pl.when(odd == 1)
    def _():
        for c in range(NCH):
            piece(0, 1, 1, c, (sib, p)).start()

    def forward2(c):
        arrived(2, c)

        @pl.when(fwd_go)
        def _():
            piece(2, 3, 3, c, fwd_to).start()

        @pl.when(odd == 1)
        def _():
            piece(2, 3, 2, c, (sib, p)).start()

        @pl.when(even == 1)
        def _():
            piece(2, 1, 2, c, (sib, p)).start()

        @pl.when(chain2)
        def _():
            piece(2, 2, 4, c, (m, chain_next)).start()

    def forward3(c):
        @pl.when(chain3)
        def _():
            arrived(3, c)
            piece(3, 3, 5, c, (m, chain_next)).start()

    def split(both):
        cr, ci = both[:FR, :LB], both[:FR, LB:]
        sr, si = both[FR:, :LB], both[FR:, LB:]
        return cr + si, ci - sr, cr - si, ci + sr

    def tspec(s):
        trow[...] = jnp.dot(rowf[:, :TS], slots[s, :TS, :], preferred_element_type=F32).astype(BF16)
        for j in range(NB):
            ar, ai, br, bi = split(jnp.dot(trow[...], colf[j, :TS, :], preferred_element_type=F32))
            tbuf[s, j, :FR, :LB] = ar
            tbuf[s, j, :FR, LB:] = ai
            tbuf[s, j, FR:, :LB] = br
            tbuf[s, j, FR:, LB:] = bi

    def mspectrum():
        @pl.when(halo_come)
        def _():
            halo_copy().wait_recv()
        urow[:, TC:] = jnp.dot(rowf[:, :MR], halo[...], preferred_element_type=F32).astype(BF16)
        bin_id = bins_ref[0]
        lane = lax.broadcasted_iota(jnp.int32, (FR, 128), 1)
        rs = jnp.sum(jnp.where(lane == bin_id, rtab[...], 0.0), axis=1, keepdims=True)
        rc = jnp.sum(jnp.where(lane == bin_id + NBINS, rtab[...], 0.0), axis=1, keepdims=True)
        which = lax.broadcasted_iota(jnp.int32, (2 * NBINS, HALF), 0)
        cc = jnp.sum(jnp.where(which == bin_id, ctab[...], 0.0), axis=0, keepdims=True)
        cs = jnp.sum(jnp.where(which == bin_id + NBINS, ctab[...], 0.0), axis=0, keepdims=True)
        for j in range(NB):
            ctf = rs * cc[:, j * LB:(j + 1) * LB] + rc * cs[:, j * LB:(j + 1) * LB]
            ar, ai, br, bi = split(jnp.dot(urow[...], colf[j], preferred_element_type=F32))
            mspec[j, :FR, :LB] = ar * ctf
            mspec[j, :FR, LB:] = ai * ctf
            mspec[j, FR:, :LB] = br * ctf
            mspec[j, FR:, LB:] = bi * ctf

    def match(s, first):
        corr = None
        for j in range(NB):
            mr, mi = mspec[j, :, :LB], mspec[j, :, LB:]
            tr, ti = tbuf[s, j, :, :LB], tbuf[s, j, :, LB:]
            prod[j, :, :LB] = (mr * tr + mi * ti).astype(BF16)
            prod[j, :, LB:] = (mi * tr - mr * ti).astype(BF16)
            both = jnp.dot(rowi[...], prod[j], preferred_element_type=F32)
            real = both[:MH, :LB] - both[MH:, LB:]
            imag = both[:MH, LB:] + both[MH:, :LB]
            back = jnp.concatenate([real, imag], axis=1).astype(BF16)
            part = jnp.dot(back, coli[j], preferred_element_type=F32)
            corr = part if corr is None else corr + part
        corr = corr * (1.0 / (TS * LR * LC))
        x = 2.0 * corr
        weight = jnp.maximum(x, 0.0) + jnp.log1p(jnp.exp(-jnp.abs(x)))
        pair = slots[s, TS:, :].astype(F32)
        wc, ws = weight * pair[0:1], weight * pair[8:9]
        if first:
            fresh = (corr, corr, corr * corr, weight, wc, ws)
        else:
            fresh = (jnp.maximum(out_ref[0], corr), out_ref[1] + corr, out_ref[2] + corr * corr,
                     out_ref[3] + weight, out_ref[4] + wc, out_ref[5] + ws)
        for n, value in enumerate(fresh):
            out_ref[n] = value

    for load in loads[1:]:
        load.wait()
    urow[:, :TC] = jnp.dot(rowf[:, :MR], own[...], preferred_element_type=F32).astype(BF16)
    tspec(0)

    @pl.when(even == 1)
    def _():
        for c in range(NCH):
            arrived(1, c)
        tspec(1)

    @pl.when(high2)
    def _():
        mspectrum()

    for c in range(NCH):
        forward2(c)

    @pl.when(jnp.logical_not(high2))
    def _():
        mspectrum()

    forward3(0)
    tspec(2)
    forward3(1)
    match(0, True)
    match(2, False)
    forward3(2)

    @pl.when(odd == 1)
    def _():
        for c in range(NCH):
            arrived(1, c)
        tspec(1)

    forward3(3)
    match(1, False)
    for c in range(4, NCH):
        forward3(c)

    @pl.when(jnp.logical_not(chain3))
    def _():
        for c in range(NCH):
            arrived(3, c)

    tspec(3)
    match(3, False)

    @pl.when(halo_go)
    def _():
        halo_copy().wait_send()

    for go, src, dst, sem, to in (
        (own_go, 0, 2, 0, own_to), (odd == 1, 0, 1, 1, (sib, p)), (fwd_go, 2, 3, 3, fwd_to),
        (odd == 1, 2, 3, 2, (sib, p)), (even == 1, 2, 1, 2, (sib, p)),
        (chain2, 2, 2, 4, (m, chain_next)), (chain3, 3, 3, 5, (m, chain_next)),
    ):
        @pl.when(go)
        def _(src=src, dst=dst, sem=sem, to=to):
            for c in range(NCH):
                piece(src, dst, sem, c, to).wait_send()


def body(mics, tiles, consts, micrograph, templates, orient_ids, defocus_bins):
    hbm = pl.BlockSpec(memory_space=pltpu.HBM)
    smem = pl.BlockSpec(memory_space=pltpu.SMEM)
    stats = pl.pallas_call(
        functools.partial(kernel, mics, tiles),
        out_shape=jax.ShapeDtypeStruct((6, MH, TC), F32),
        in_specs=[hbm, hbm, smem, smem] + [hbm] * 6,
        out_specs=pl.BlockSpec(memory_space=pltpu.VMEM),
        scratch_shapes=[
            pltpu.VMEM((NB, LC, 2 * LB), BF16),
            pltpu.VMEM((2 * FR, LR), BF16),
            pltpu.VMEM((2 * MH, 2 * FR), BF16),
            pltpu.VMEM((NB, 2 * LB, TC), BF16),
            pltpu.VMEM((FR, 128), F32),
            pltpu.VMEM((2 * NBINS, HALF), F32),
            pltpu.VMEM((MR, TC), BF16),
            pltpu.VMEM((MR, TC), BF16),
            pltpu.VMEM((STEPS, SLOT, TS), BF16),
            pltpu.VMEM((2 * FR, 2 * TC), BF16),
            pltpu.VMEM((2 * FR, TS), BF16),
            pltpu.VMEM((NB, 2 * FR, 2 * LB), F32),
            pltpu.VMEM((STEPS, NB, 2 * FR, 2 * LB), F32),
            pltpu.VMEM((NB, 2 * FR, 2 * LB), BF16),
            pltpu.SemaphoreType.DMA((8,)),
            pltpu.SemaphoreType.DMA,
            pltpu.SemaphoreType.DMA,
            pltpu.SemaphoreType.DMA((6, NCH)),
            pltpu.SemaphoreType.DMA((3, NCH)),
        ],
        compiler_params=pltpu.CompilerParams(
            collective_id=0, has_side_effects=True, vmem_limit_bytes=56 * 1024 * 1024),
    )(micrograph, templates, orient_ids, defocus_bins, *consts)
    results = (stats[0], stats[1], stats[2], stats[4] / stats[3], stats[5] / stats[3])
    return tuple(value[None] for value in results)


def solution(mesh):
    placed = (P("mic", None, "tile"), P("mic", None, None), P("mic"), P("mic"))
    consts = tuple(jnp.asarray(table) for table in tables())
    return jax.shard_map(
        functools.partial(body, mesh.shape["mic"], mesh.shape["tile"], consts),
        mesh=mesh,
        in_specs=placed,
        out_specs=(P("mic", None, "tile"),) * 5,
        check_vma=False,
    )
```

```python
import functools
import math

import jax
import jax.numpy as jnp
import ml_dtypes
import numpy as np
from jax import lax
from jax.experimental import pallas as pl
from jax.experimental.pallas import tpu as pltpu
from jax.sharding import PartitionSpec as P

TS = 384
TC = 384
MH = 64
STEPS = 4
NANG = 360
NBINS = 16
MR = 447
MC = 767
LR = 448
LC = 768
HALF = 384
FOLD = 225
FR = 240
NB = 3
LB = 128
SLOT = 400
CHUNKS = ((0, 64), (64, 64), (128, 64), (192, 64), (256, 64), (320, 80))
NCH = len(CHUNKS)

AMPLITUDE = 0.07
WAVELENGTH = 0.0197
BASE_DEFOCUS = 8000.0
DEFOCUS_STEP = 1000.0
MESH = pl.DeviceIdType.MESH
BF16 = jnp.bfloat16
F32 = jnp.float32


def trig(left, right, length):
    ids = (np.arange(left)[:, None] * np.arange(right)[None, :]) % length
    angles = ids.astype(np.float32) * np.float32(2.0 * math.pi / length)
    return np.cos(angles), np.sin(angles)


def tables():
    bf16 = ml_dtypes.bfloat16
    c, s = trig(LC, HALF, LC)
    c[MC:], s[MC:] = 0.0, 0.0
    colf = np.stack([np.concatenate([c[:, j * LB:(j + 1) * LB], -s[:, j * LB:(j + 1) * LB]], 1) for j in range(NB)])
    c, s = trig(FOLD, LR, LR)
    rowf = np.zeros((2 * FR, LR), np.float32)
    rowf[:FOLD, :MR] = c[:, :MR]
    rowf[FR:FR + FOLD, :MR] = s[:, :MR]
    c, s = trig(MH, FOLD, LR)
    rowi = np.zeros((2 * MH, 2 * FR), np.float32)
    rowi[:MH, :FOLD] = c
    rowi[MH:, :FOLD] = s
    rowi[:MH, FR + 1:FR + FOLD - 1] = c[:, 1:FOLD - 1]
    rowi[MH:, FR + 1:FR + FOLD - 1] = -s[:, 1:FOLD - 1]
    c, s = trig(HALF, TC, LC)
    w = np.where(np.arange(HALF) == 0, 1.0, 2.0).astype(np.float32)[:, None]
    c, s = c * w, s * w
    coli = np.stack([np.concatenate([c[j * LB:(j + 1) * LB], -s[j * LB:(j + 1) * LB]], 0) for j in range(NB)])
    scale = math.pi * WAVELENGTH * (BASE_DEFOCUS + DEFOCUS_STEP * np.arange(NBINS))
    phi = math.atan2(AMPLITUDE, math.sqrt(1.0 - AMPLITUDE * AMPLITUDE))
    rows = scale[None, :] * (np.arange(FOLD)[:, None] / LR) ** 2 + phi
    rtab = np.zeros((FR, 128), np.float32)
    rtab[:FOLD, :NBINS] = -np.sin(rows)
    rtab[:FOLD, NBINS:2 * NBINS] = -np.cos(rows)
    cols = scale[:, None] * (np.arange(HALF)[None, :] / LC) ** 2
    ctab = np.concatenate([np.cos(cols), np.sin(cols)], 0).astype(np.float32)
    return (colf.astype(bf16), rowf.astype(bf16), rowi.astype(bf16), coli.astype(bf16), rtab, ctab)


def kernel(mics, tiles, mic_ref, tmpl_ref, orient_ref, bins_ref, colf_h, rowf_h, rowi_h, coli_h, rtab_h, ctab_h,
           out_ref, colf, rowf, rowi, coli, rtab, ctab, own, halo, slots, urow, trow, mspec, tbuf, prod,
           lsem, hsend, hrecv, ssem, rsem):
    m = lax.axis_index("mic")
    p = lax.axis_index("tile")
    group = mics // 2
    mg = lax.rem(m, group)
    odd = lax.rem(m, 2)
    even = 1 - odd
    sib = m + 1 - 2 * odd
    down1 = lax.rem(m + mics - 1, mics)
    down2 = lax.rem(m + mics - 2, mics)
    up1 = lax.rem(m + 1, mics)
    up2 = lax.rem(m + 2, mics)
    last = tiles - 1
    upper_half = m >= group
    low2 = mg < 2
    low1 = mg == 0
    high2 = mg >= group - 2
    high1 = mg == group - 1

    edge_tile = jnp.logical_or(p == 0, p == last)
    exit_tile = edge_tile
    entry_tile = edge_tile
    chain_next = jnp.where(p == 0, 1, last - 1)
    chain_prev = jnp.where(p == 1, 0, last)
    chain_p = edge_tile
    own_go = jnp.logical_or(jnp.logical_not(low2), exit_tile)
    own_to = (down2, jnp.where(low2, last - p, p))
    fwd_go = jnp.logical_and(even == 1, jnp.logical_or(jnp.logical_not(low1), exit_tile))
    fwd_to = (down1, jnp.where(low1, last - p, p))
    chain2 = jnp.logical_and(high2, chain_p)
    chain3 = jnp.logical_and(high1, chain_p)
    halo_go = p > 0
    halo_come = p < last
    next_tile = jnp.minimum(p + 1, last)
    prev_tile = jnp.maximum(p - 1, 0)

    loads = [
        pltpu.make_async_copy(tmpl_ref.at[0], slots.at[0, pl.ds(0, TS)], lsem.at[0]),
        pltpu.make_async_copy(mic_ref.at[0], own, lsem.at[1]),
        pltpu.make_async_copy(colf_h, colf, lsem.at[2]),
        pltpu.make_async_copy(rowf_h, rowf, lsem.at[3]),
        pltpu.make_async_copy(rtab_h, rtab, lsem.at[4]),
        pltpu.make_async_copy(ctab_h, ctab, lsem.at[5]),
        pltpu.make_async_copy(rowi_h, rowi, lsem.at[6]),
        pltpu.make_async_copy(coli_h, coli, lsem.at[7]),
    ]
    for load in loads:
        load.start()

    barrier = pltpu.get_barrier_semaphore()

    def greet(to):
        pl.semaphore_signal(barrier, inc=1, device_id=to, device_id_type=MESH)

    greet((sib, p))
    inner_high2 = jnp.logical_and(high2, jnp.logical_not(entry_tile))
    inner_high1 = jnp.logical_and(high1, jnp.logical_not(entry_tile))

    @pl.when(inner_high2)
    def _():
        greet((m, chain_prev))

    @pl.when(jnp.logical_not(inner_high2))
    def _():
        greet((up2, jnp.where(high2, last - p, p)))

    @pl.when(inner_high1)
    def _():
        greet((m, chain_prev))

    @pl.when(jnp.logical_and(odd == 1, jnp.logical_not(inner_high1)))
    def _():
        greet((up1, jnp.where(high1, last - p, p)))

    @pl.when(halo_come)
    def _():
        greet((m, next_tile))

    @pl.when(jnp.logical_not(halo_come))
    def _():
        halo[...] = jnp.zeros_like(halo)

    angle = jnp.full((16, TS), orient_ref[0], jnp.int32).astype(F32) * (2.0 * math.pi / NANG)
    upper = lax.broadcasted_iota(jnp.int32, (16, TS), 0) < 8
    slots[0, TS:, :] = jnp.where(upper, jnp.cos(angle), jnp.sin(angle)).astype(BF16)

    i32 = lambda b: b.astype(jnp.int32)
    pl.semaphore_wait(barrier, 1 + i32(own_go) + i32(fwd_go) + i32(halo_go) + i32(chain2) + i32(chain3))

    def halo_copy():
        return pltpu.make_async_remote_copy(
            src_ref=mic_ref.at[0], dst_ref=halo, send_sem=hsend, recv_sem=hrecv,
            device_id=(m, prev_tile), device_id_type=MESH)

    def piece(src, dst, sem, chunk, to):
        start, rows = CHUNKS[chunk]
        return pltpu.make_async_remote_copy(
            src_ref=slots.at[src, pl.ds(start, rows)], dst_ref=slots.at[dst, pl.ds(start, rows)],
            send_sem=ssem.at[sem, chunk], recv_sem=rsem.at[dst - 1, chunk],
            device_id=to, device_id_type=MESH)

    def arrived(slot, chunk):
        piece(slot, slot, 0, chunk, (sib, p)).wait_recv()

    @pl.when(halo_go)
    def _():
        halo_copy().start()

    loads[0].wait()

    @pl.when(own_go)
    def _():
        for c in range(NCH):
            piece(0, 2, 0, c, own_to).start()

    @pl.when(odd == 1)
    def _():
        for c in range(NCH):
            piece(0, 1, 1, c, (sib, p)).start()

    def forward2(c):
        arrived(2, c)

        @pl.when(fwd_go)
        def _():
            piece(2, 3, 3, c, fwd_to).start()

        @pl.when(odd == 1)
        def _():
            piece(2, 3, 2, c, (sib, p)).start()

        @pl.when(even == 1)
        def _():
            piece(2, 1, 2, c, (sib, p)).start()

        @pl.when(chain2)
        def _():
            piece(2, 2, 4, c, (m, chain_next)).start()

    def forward3(c):
        @pl.when(chain3)
        def _():
            arrived(3, c)
            piece(3, 3, 5, c, (m, chain_next)).start()

    def split(both):
        cr, ci = both[:FR, :LB], both[:FR, LB:]
        sr, si = both[FR:, :LB], both[FR:, LB:]
        return cr + si, ci - sr, cr - si, ci + sr

    def tspec(s):
        trow[...] = jnp.dot(rowf[:, :TS], slots[s, :TS, :], preferred_element_type=F32).astype(BF16)
        for j in range(NB):
            ar, ai, br, bi = split(jnp.dot(trow[...], colf[j, :TS, :], preferred_element_type=F32))
            tbuf[s, j, :FR, :LB] = ar
            tbuf[s, j, :FR, LB:] = ai
            tbuf[s, j, FR:, :LB] = br
            tbuf[s, j, FR:, LB:] = bi

    def mspectrum():
        @pl.when(halo_come)
        def _():
            halo_copy().wait_recv()
        urow[:, TC:] = jnp.dot(rowf[:, :MR], halo[...], preferred_element_type=F32).astype(BF16)
        bin_id = bins_ref[0]
        lane = lax.broadcasted_iota(jnp.int32, (FR, 128), 1)
        rs = jnp.sum(jnp.where(lane == bin_id, rtab[...], 0.0), axis=1, keepdims=True)
        rc = jnp.sum(jnp.where(lane == bin_id + NBINS, rtab[...], 0.0), axis=1, keepdims=True)
        which = lax.broadcasted_iota(jnp.int32, (2 * NBINS, HALF), 0)
        cc = jnp.sum(jnp.where(which == bin_id, ctab[...], 0.0), axis=0, keepdims=True)
        cs = jnp.sum(jnp.where(which == bin_id + NBINS, ctab[...], 0.0), axis=0, keepdims=True)
        for j in range(NB):
            ctf = rs * cc[:, j * LB:(j + 1) * LB] + rc * cs[:, j * LB:(j + 1) * LB]
            ar, ai, br, bi = split(jnp.dot(urow[...], colf[j], preferred_element_type=F32))
            mspec[j, :FR, :LB] = ar * ctf
            mspec[j, :FR, LB:] = ai * ctf
            mspec[j, FR:, :LB] = br * ctf
            mspec[j, FR:, LB:] = bi * ctf

    def match(s, first):
        corr = None
        for j in range(NB):
            mr, mi = mspec[j, :, :LB], mspec[j, :, LB:]
            tr, ti = tbuf[s, j, :, :LB], tbuf[s, j, :, LB:]
            prod[j, :, :LB] = (mr * tr + mi * ti).astype(BF16)
            prod[j, :, LB:] = (mi * tr - mr * ti).astype(BF16)
            both = jnp.dot(rowi[...], prod[j], preferred_element_type=F32)
            real = both[:MH, :LB] - both[MH:, LB:]
            imag = both[:MH, LB:] + both[MH:, :LB]
            back = jnp.concatenate([real, imag], axis=1).astype(BF16)
            part = jnp.dot(back, coli[j], preferred_element_type=F32)
            corr = part if corr is None else corr + part
        corr = corr * (1.0 / (TS * LR * LC))
        x = 2.0 * corr
        weight = jnp.maximum(x, 0.0) + jnp.log1p(jnp.exp(-jnp.abs(x)))
        pair = slots[s, TS:, :].astype(F32)
        wc, ws = weight * pair[0:1], weight * pair[8:9]
        if first:
            fresh = (corr, corr, corr * corr, weight, wc, ws)
        else:
            fresh = (jnp.maximum(out_ref[0], corr), out_ref[1] + corr, out_ref[2] + corr * corr,
                     out_ref[3] + weight, out_ref[4] + wc, out_ref[5] + ws)
        for n, value in enumerate(fresh):
            out_ref[n] = value

    for load in loads[1:]:
        load.wait()
    urow[:, :TC] = jnp.dot(rowf[:, :MR], own[...], preferred_element_type=F32).astype(BF16)
    tspec(0)

    @pl.when(even == 1)
    def _():
        for c in range(NCH):
            arrived(1, c)
        tspec(1)

    def arrived_all(slot):
        for c in range(NCH):
            arrived(slot, c)

    @pl.when(high2)
    def _():
        mspectrum()
        match(0, True)
        for c in range(NCH):
            forward2(c)
        tspec(2)
        forward3(0)
        forward3(1)
        forward3(2)
        match(2, False)
        for c in range(3, NCH):
            forward3(c)

        @pl.when(odd == 1)
        def _():
            arrived_all(1)
            tspec(1)

        match(1, False)

    @pl.when(jnp.logical_not(high2))
    def _():
        for c in range(NCH):
            forward2(c)
        tspec(2)

        @pl.when(odd == 1)
        def _():
            arrived_all(1)
            tspec(1)

        mspectrum()
        match(0, True)
        match(1, False)
        match(2, False)

    @pl.when(jnp.logical_not(chain3))
    def _():
        arrived_all(3)

    tspec(3)
    match(3, False)

    @pl.when(halo_go)
    def _():
        halo_copy().wait_send()

    for go, src, dst, sem, to in (
        (own_go, 0, 2, 0, own_to), (odd == 1, 0, 1, 1, (sib, p)), (fwd_go, 2, 3, 3, fwd_to),
        (odd == 1, 2, 3, 2, (sib, p)), (even == 1, 2, 1, 2, (sib, p)),
        (chain2, 2, 2, 4, (m, chain_next)), (chain3, 3, 3, 5, (m, chain_next)),
    ):
        @pl.when(go)
        def _(src=src, dst=dst, sem=sem, to=to):
            for c in range(NCH):
                piece(src, dst, sem, c, to).wait_send()


def body(mics, tiles, consts, micrograph, templates, orient_ids, defocus_bins):
    hbm = pl.BlockSpec(memory_space=pltpu.HBM)
    smem = pl.BlockSpec(memory_space=pltpu.SMEM)
    stats = pl.pallas_call(
        functools.partial(kernel, mics, tiles),
        out_shape=jax.ShapeDtypeStruct((6, MH, TC), F32),
        in_specs=[hbm, hbm, smem, smem] + [hbm] * 6,
        out_specs=pl.BlockSpec(memory_space=pltpu.VMEM),
        scratch_shapes=[
            pltpu.VMEM((NB, LC, 2 * LB), BF16),
            pltpu.VMEM((2 * FR, LR), BF16),
            pltpu.VMEM((2 * MH, 2 * FR), BF16),
            pltpu.VMEM((NB, 2 * LB, TC), BF16),
            pltpu.VMEM((FR, 128), F32),
            pltpu.VMEM((2 * NBINS, HALF), F32),
            pltpu.VMEM((MR, TC), BF16),
            pltpu.VMEM((MR, TC), BF16),
            pltpu.VMEM((STEPS, SLOT, TS), BF16),
            pltpu.VMEM((2 * FR, 2 * TC), BF16),
            pltpu.VMEM((2 * FR, TS), BF16),
            pltpu.VMEM((NB, 2 * FR, 2 * LB), F32),
            pltpu.VMEM((STEPS, NB, 2 * FR, 2 * LB), F32),
            pltpu.VMEM((NB, 2 * FR, 2 * LB), BF16),
            pltpu.SemaphoreType.DMA((8,)),
            pltpu.SemaphoreType.DMA,
            pltpu.SemaphoreType.DMA,
            pltpu.SemaphoreType.DMA((6, NCH)),
            pltpu.SemaphoreType.DMA((3, NCH)),
        ],
        compiler_params=pltpu.CompilerParams(
            collective_id=0, has_side_effects=True, vmem_limit_bytes=52 * 1024 * 1024),
    )(*[pltpu.with_memory_space_constraint(a, pltpu.HBM) for a in (micrograph, templates)], orient_ids, defocus_bins, *[pltpu.with_memory_space_constraint(a, pltpu.HBM) for a in consts])
    results = (stats[0], stats[1], stats[2], stats[4] / stats[3], stats[5] / stats[3])
    return tuple(value[None] for value in results)


def solution(mesh):
    placed = (P("mic", None, "tile"), P("mic", None, None), P("mic"), P("mic"))
    consts = tuple(jnp.asarray(table) for table in tables())
    return jax.shard_map(
        functools.partial(body, mesh.shape["mic"], mesh.shape["tile"], consts),
        mesh=mesh,
        in_specs=placed,
        out_specs=(P("mic", None, "tile"),) * 5,
        check_vma=False,
    )
```

```python
import functools
import math

import jax
import jax.numpy as jnp
import ml_dtypes
import numpy as np
from jax import lax
from jax.experimental import pallas as pl
from jax.experimental.pallas import tpu as pltpu
from jax.sharding import PartitionSpec as P

TS = 384
TC = 384
MH = 64
STEPS = 4
NANG = 360
NBINS = 16
MR = 447
MC = 767
LR = 448
LC = 768
HALF = 384
FOLD = 225
FR = 240
NB = 3
LB = 128
SLOT = 400
CHUNKS = ((0, 64), (64, 64), (128, 64), (192, 64), (256, 64), (320, 80))
NCH = len(CHUNKS)

AMPLITUDE = 0.07
WAVELENGTH = 0.0197
BASE_DEFOCUS = 8000.0
DEFOCUS_STEP = 1000.0
MESH = pl.DeviceIdType.MESH
BF16 = jnp.bfloat16
F32 = jnp.float32


def trig(left, right, length):
    ids = (np.arange(left)[:, None] * np.arange(right)[None, :]) % length
    angles = ids.astype(np.float32) * np.float32(2.0 * math.pi / length)
    return np.cos(angles), np.sin(angles)


def tables():
    bf16 = ml_dtypes.bfloat16
    c, s = trig(LC, HALF, LC)
    c[MC:], s[MC:] = 0.0, 0.0
    colf = np.stack([np.concatenate([c[:, j * LB:(j + 1) * LB], -s[:, j * LB:(j + 1) * LB]], 1) for j in range(NB)])
    c, s = trig(FOLD, LR, LR)
    rowf = np.zeros((2 * FR, LR), np.float32)
    rowf[:FOLD, :MR] = c[:, :MR]
    rowf[FR:FR + FOLD, :MR] = s[:, :MR]
    c, s = trig(MH, FOLD, LR)
    rowi = np.zeros((2 * MH, 2 * FR), np.float32)
    rowi[:MH, :FOLD] = c
    rowi[MH:, :FOLD] = s
    rowi[:MH, FR + 1:FR + FOLD - 1] = c[:, 1:FOLD - 1]
    rowi[MH:, FR + 1:FR + FOLD - 1] = -s[:, 1:FOLD - 1]
    c, s = trig(HALF, TC, LC)
    w = np.where(np.arange(HALF) == 0, 1.0, 2.0).astype(np.float32)[:, None]
    c, s = c * w, s * w
    coli = np.stack([np.concatenate([c[j * LB:(j + 1) * LB], -s[j * LB:(j + 1) * LB]], 0) for j in range(NB)])
    scale = math.pi * WAVELENGTH * (BASE_DEFOCUS + DEFOCUS_STEP * np.arange(NBINS))
    phi = math.atan2(AMPLITUDE, math.sqrt(1.0 - AMPLITUDE * AMPLITUDE))
    rows = scale[None, :] * (np.arange(FOLD)[:, None] / LR) ** 2 + phi
    rtab = np.zeros((FR, 128), np.float32)
    rtab[:FOLD, :NBINS] = -np.sin(rows)
    rtab[:FOLD, NBINS:2 * NBINS] = -np.cos(rows)
    cols = scale[:, None] * (np.arange(HALF)[None, :] / LC) ** 2
    ctab = np.concatenate([np.cos(cols), np.sin(cols)], 0).astype(np.float32)
    return (colf.astype(bf16), rowf.astype(bf16), rowi.astype(bf16), coli.astype(bf16), rtab, ctab)


def kernel(mics, tiles, mic_ref, tmpl_ref, orient_ref, bins_ref, colf_h, rowf_h, rowi_h, coli_h, rtab_h, ctab_h,
           out_ref, colf, rowf, rowi, coli, rtab, ctab, own, halo, slots, urow, trow, mspec, tbuf, prod,
           lsem, hsend, hrecv, ssem, rsem):
    m = lax.axis_index("mic")
    p = lax.axis_index("tile")
    group = mics // 2
    mg = lax.rem(m, group)
    odd = lax.rem(m, 2)
    even = 1 - odd
    sib = m + 1 - 2 * odd
    down1 = lax.rem(m + mics - 1, mics)
    down2 = lax.rem(m + mics - 2, mics)
    up1 = lax.rem(m + 1, mics)
    up2 = lax.rem(m + 2, mics)
    last = tiles - 1
    upper_half = m >= group
    low2 = mg < 2
    low1 = mg == 0
    high2 = mg >= group - 2
    high1 = mg == group - 1

    edge_tile = jnp.logical_or(p == 0, p == last)
    exit_tile = edge_tile
    entry_tile = edge_tile
    chain_next = jnp.where(p == 0, 1, last - 1)
    chain_prev = jnp.where(p == 1, 0, last)
    chain_p = edge_tile
    own_go = jnp.logical_or(jnp.logical_not(low2), exit_tile)
    own_to = (down2, jnp.where(low2, last - p, p))
    fwd_go = jnp.logical_and(even == 1, jnp.logical_or(jnp.logical_not(low1), exit_tile))
    fwd_to = (down1, jnp.where(low1, last - p, p))
    chain2 = jnp.logical_and(high2, chain_p)
    chain3 = jnp.logical_and(high1, chain_p)
    halo_go = p > 0
    halo_come = p < last
    next_tile = jnp.minimum(p + 1, last)
    prev_tile = jnp.maximum(p - 1, 0)

    loads = [
        pltpu.make_async_copy(tmpl_ref.at[0], slots.at[0, pl.ds(0, TS)], lsem.at[0]),
        pltpu.make_async_copy(mic_ref.at[0], own, lsem.at[1]),
        pltpu.make_async_copy(colf_h, colf, lsem.at[2]),
        pltpu.make_async_copy(rowf_h, rowf, lsem.at[3]),
        pltpu.make_async_copy(rtab_h, rtab, lsem.at[4]),
        pltpu.make_async_copy(ctab_h, ctab, lsem.at[5]),
        pltpu.make_async_copy(rowi_h, rowi, lsem.at[6]),
        pltpu.make_async_copy(coli_h, coli, lsem.at[7]),
    ]
    for load in loads:
        load.start()

    barrier = pltpu.get_barrier_semaphore()

    def greet(to):
        pl.semaphore_signal(barrier, inc=1, device_id=to, device_id_type=MESH)

    greet((sib, p))
    inner_high2 = jnp.logical_and(high2, jnp.logical_not(entry_tile))
    inner_high1 = jnp.logical_and(high1, jnp.logical_not(entry_tile))

    @pl.when(inner_high2)
    def _():
        greet((m, chain_prev))

    @pl.when(jnp.logical_not(inner_high2))
    def _():
        greet((up2, jnp.where(high2, last - p, p)))

    @pl.when(inner_high1)
    def _():
        greet((m, chain_prev))

    @pl.when(jnp.logical_and(odd == 1, jnp.logical_not(inner_high1)))
    def _():
        greet((up1, jnp.where(high1, last - p, p)))

    @pl.when(halo_come)
    def _():
        greet((m, next_tile))

    @pl.when(jnp.logical_not(halo_come))
    def _():
        halo[...] = jnp.zeros_like(halo)

    angle = jnp.full((16, TS), orient_ref[0], jnp.int32).astype(F32) * (2.0 * math.pi / NANG)
    upper = lax.broadcasted_iota(jnp.int32, (16, TS), 0) < 8
    slots[0, TS:, :] = jnp.where(upper, jnp.cos(angle), jnp.sin(angle)).astype(BF16)

    i32 = lambda b: b.astype(jnp.int32)
    pl.semaphore_wait(barrier, 1 + i32(own_go) + i32(fwd_go) + i32(halo_go) + i32(chain2) + i32(chain3))

    def halo_copy():
        return pltpu.make_async_remote_copy(
            src_ref=mic_ref.at[0], dst_ref=halo, send_sem=hsend, recv_sem=hrecv,
            device_id=(m, prev_tile), device_id_type=MESH)

    def piece(src, dst, sem, chunk, to):
        start, rows = CHUNKS[chunk]
        return pltpu.make_async_remote_copy(
            src_ref=slots.at[src, pl.ds(start, rows)], dst_ref=slots.at[dst, pl.ds(start, rows)],
            send_sem=ssem.at[sem, chunk], recv_sem=rsem.at[dst - 1, chunk],
            device_id=to, device_id_type=MESH)

    def arrived(slot, chunk):
        piece(slot, slot, 0, chunk, (sib, p)).wait_recv()

    @pl.when(halo_go)
    def _():
        halo_copy().start()

    loads[0].wait()

    @pl.when(own_go)
    def _():
        for c in range(NCH):
            piece(0, 2, 0, c, own_to).start()

    @pl.when(odd == 1)
    def _():
        for c in range(NCH):
            piece(0, 1, 1, c, (sib, p)).start()

    def forward2(c):
        arrived(2, c)

        @pl.when(fwd_go)
        def _():
            piece(2, 3, 3, c, fwd_to).start()

        @pl.when(odd == 1)
        def _():
            piece(2, 3, 2, c, (sib, p)).start()

        @pl.when(even == 1)
        def _():
            piece(2, 1, 2, c, (sib, p)).start()

        @pl.when(chain2)
        def _():
            piece(2, 2, 4, c, (m, chain_next)).start()

    def forward3(c):
        @pl.when(chain3)
        def _():
            arrived(3, c)
            piece(3, 3, 5, c, (m, chain_next)).start()

    def split(both):
        cr, ci = both[:FR, :LB], both[:FR, LB:]
        sr, si = both[FR:, :LB], both[FR:, LB:]
        return cr + si, ci - sr, cr - si, ci + sr

    def tspec(s):
        trow[...] = jnp.dot(rowf[:, :TS], slots[s, :TS, :], preferred_element_type=F32).astype(BF16)
        for j in range(NB):
            ar, ai, br, bi = split(jnp.dot(trow[...], colf[j, :TS, :], preferred_element_type=F32))
            tbuf[s, j, :FR, :LB] = ar
            tbuf[s, j, :FR, LB:] = ai
            tbuf[s, j, FR:, :LB] = br
            tbuf[s, j, FR:, LB:] = bi

    def mspectrum():
        @pl.when(halo_come)
        def _():
            halo_copy().wait_recv()
        urow[:, TC:] = jnp.dot(rowf[:, :MR], halo[...], preferred_element_type=F32).astype(BF16)
        bin_id = bins_ref[0]
        lane = lax.broadcasted_iota(jnp.int32, (FR, 128), 1)
        rs = jnp.sum(jnp.where(lane == bin_id, rtab[...], 0.0), axis=1, keepdims=True)
        rc = jnp.sum(jnp.where(lane == bin_id + NBINS, rtab[...], 0.0), axis=1, keepdims=True)
        which = lax.broadcasted_iota(jnp.int32, (2 * NBINS, HALF), 0)
        cc = jnp.sum(jnp.where(which == bin_id, ctab[...], 0.0), axis=0, keepdims=True)
        cs = jnp.sum(jnp.where(which == bin_id + NBINS, ctab[...], 0.0), axis=0, keepdims=True)
        for j in range(NB):
            ctf = rs * cc[:, j * LB:(j + 1) * LB] + rc * cs[:, j * LB:(j + 1) * LB]
            ar, ai, br, bi = split(jnp.dot(urow[...], colf[j], preferred_element_type=F32))
            mspec[j, :FR, :LB] = ar * ctf
            mspec[j, :FR, LB:] = ai * ctf
            mspec[j, FR:, :LB] = br * ctf
            mspec[j, FR:, LB:] = bi * ctf

    def match(s, first):
        corr = None
        for j in range(NB):
            mr, mi = mspec[j, :, :LB], mspec[j, :, LB:]
            tr, ti = tbuf[s, j, :, :LB], tbuf[s, j, :, LB:]
            prod[j, :, :LB] = (mr * tr + mi * ti).astype(BF16)
            prod[j, :, LB:] = (mi * tr - mr * ti).astype(BF16)
            both = jnp.dot(rowi[...], prod[j], preferred_element_type=F32)
            real = both[:MH, :LB] - both[MH:, LB:]
            imag = both[:MH, LB:] + both[MH:, :LB]
            back = jnp.concatenate([real, imag], axis=1).astype(BF16)
            part = jnp.dot(back, coli[j], preferred_element_type=F32)
            corr = part if corr is None else corr + part
        corr = corr * (1.0 / (TS * LR * LC))
        x = 2.0 * corr
        weight = jnp.maximum(x, 0.0) + jnp.log1p(jnp.exp(-jnp.abs(x)))
        pair = slots[s, TS:, :].astype(F32)
        wc, ws = weight * pair[0:1], weight * pair[8:9]
        if first:
            fresh = (corr, corr, corr * corr, weight, wc, ws)
        else:
            fresh = (jnp.maximum(out_ref[0], corr), out_ref[1] + corr, out_ref[2] + corr * corr,
                     out_ref[3] + weight, out_ref[4] + wc, out_ref[5] + ws)
        for n, value in enumerate(fresh):
            out_ref[n] = value

    for load in loads[1:]:
        load.wait()
    urow[:, :TC] = jnp.dot(rowf[:, :MR], own[...], preferred_element_type=F32).astype(BF16)
    @pl.when(low1)
    def _():
        for c in range(NCH):
            forward2(c)

    tspec(0)

    @pl.when(even == 1)
    def _():
        for c in range(NCH):
            arrived(1, c)
        tspec(1)

    def arrived_all(slot):
        for c in range(NCH):
            arrived(slot, c)

    @pl.when(high2)
    def _():
        mspectrum()
        match(0, True)
        for c in range(NCH):
            forward2(c)
        tspec(2)
        forward3(0)
        forward3(1)
        forward3(2)
        match(2, False)
        for c in range(3, NCH):
            forward3(c)

        @pl.when(odd == 1)
        def _():
            arrived_all(1)
            tspec(1)

        match(1, False)

    @pl.when(jnp.logical_not(high2))
    def _():
        @pl.when(jnp.logical_not(low1))
        def _():
            for c in range(NCH):
                forward2(c)

        tspec(2)

        @pl.when(odd == 1)
        def _():
            arrived_all(1)
            tspec(1)

        mspectrum()
        match(0, True)
        match(1, False)
        match(2, False)

    @pl.when(jnp.logical_not(chain3))
    def _():
        arrived_all(3)

    tspec(3)
    match(3, False)

    @pl.when(halo_go)
    def _():
        halo_copy().wait_send()

    for go, src, dst, sem, to in (
        (own_go, 0, 2, 0, own_to), (odd == 1, 0, 1, 1, (sib, p)), (fwd_go, 2, 3, 3, fwd_to),
        (odd == 1, 2, 3, 2, (sib, p)), (even == 1, 2, 1, 2, (sib, p)),
        (chain2, 2, 2, 4, (m, chain_next)), (chain3, 3, 3, 5, (m, chain_next)),
    ):
        @pl.when(go)
        def _(src=src, dst=dst, sem=sem, to=to):
            for c in range(NCH):
                piece(src, dst, sem, c, to).wait_send()


def body(mics, tiles, consts, micrograph, templates, orient_ids, defocus_bins):
    hbm = pl.BlockSpec(memory_space=pltpu.HBM)
    smem = pl.BlockSpec(memory_space=pltpu.SMEM)
    stats = pl.pallas_call(
        functools.partial(kernel, mics, tiles),
        out_shape=jax.ShapeDtypeStruct((6, MH, TC), F32),
        in_specs=[hbm, hbm, smem, smem] + [hbm] * 6,
        out_specs=pl.BlockSpec(memory_space=pltpu.VMEM),
        scratch_shapes=[
            pltpu.VMEM((NB, LC, 2 * LB), BF16),
            pltpu.VMEM((2 * FR, LR), BF16),
            pltpu.VMEM((2 * MH, 2 * FR), BF16),
            pltpu.VMEM((NB, 2 * LB, TC), BF16),
            pltpu.VMEM((FR, 128), F32),
            pltpu.VMEM((2 * NBINS, HALF), F32),
            pltpu.VMEM((MR, TC), BF16),
            pltpu.VMEM((MR, TC), BF16),
            pltpu.VMEM((STEPS, SLOT, TS), BF16),
            pltpu.VMEM((2 * FR, 2 * TC), BF16),
            pltpu.VMEM((2 * FR, TS), BF16),
            pltpu.VMEM((NB, 2 * FR, 2 * LB), F32),
            pltpu.VMEM((STEPS, NB, 2 * FR, 2 * LB), F32),
            pltpu.VMEM((NB, 2 * FR, 2 * LB), BF16),
            pltpu.SemaphoreType.DMA((8,)),
            pltpu.SemaphoreType.DMA,
            pltpu.SemaphoreType.DMA,
            pltpu.SemaphoreType.DMA((6, NCH)),
            pltpu.SemaphoreType.DMA((3, NCH)),
        ],
        compiler_params=pltpu.CompilerParams(
            collective_id=0, has_side_effects=True, vmem_limit_bytes=52 * 1024 * 1024),
    )(*[pltpu.with_memory_space_constraint(a, pltpu.HBM) for a in (micrograph, templates)], orient_ids, defocus_bins, *[pltpu.with_memory_space_constraint(a, pltpu.HBM) for a in consts])
    results = (stats[0], stats[1], stats[2], stats[4] / stats[3], stats[5] / stats[3])
    return tuple(value[None] for value in results)


def solution(mesh):
    placed = (P("mic", None, "tile"), P("mic", None, None), P("mic"), P("mic"))
    consts = tuple(jnp.asarray(table) for table in tables())
    return jax.shard_map(
        functools.partial(body, mesh.shape["mic"], mesh.shape["tile"], consts),
        mesh=mesh,
        in_specs=placed,
        out_specs=(P("mic", None, "tile"),) * 5,
        check_vma=False,
    )
```
